1024 devices in a mesh: dp: 8 (over z_lo), section: 32 (over y, x, core), tensor: 4 (over z_hi).
Axes of the slice: x: 4, y: 4, z: 32 (z_hi: 4, z_lo: 8; z = z_hi * 8 + z_lo), core: 2. Of those that a mesh axis runs over, the one named last changes fastest.
Arguments:
- section_output: bfloat16 [32, 1024, 16384], P('section', 'dp', 'tensor')
- sketch_matrix: bfloat16 [32, 16384, 32], P('section', 'tensor'), may hold values from -0.046875 to 0.046875
- boundary_gain: bfloat16 [32, 16384], P('section', 'tensor'), may hold values from 0.099609375 to 1.8984375
- grad_gained: bfloat16 [32, 1024, 16384], P('section', 'dp', 'tensor')
Outputs:
- grad_output: bfloat16 [32, 1024, 16384], P('section', 'dp', 'tensor')
- gain_grad: float32 [32, 16384], P('section', 'tensor')
The draws below stay inside these ranges and needn't reach their ends.
All inputs are finite; a program needn't handle non-finite values.
Results may differ from the reference program's by a relative error of at most 0.0074.
Values may be sent and summed in bfloat16 or wider, within the bound.
No kernel may reach another device: no remote copies, remote signals or barrier semaphores. Data moves between devices by JAX's collectives and lax.ppermute only.
A program may use at most 32 MiB of HBM per device.

```python
import jax
import jax.numpy as jnp
from jax import lax

D = 16384
RANK = 32
TOK_DEV = 128
TOKENS = 1024
N_DP = 8
N_SECTION = 32
N_TENSOR = 4


def spectral_rows(key):
    key_left, key_right, key_noise = jax.random.split(key, 3)
    group_count = N_TENSOR
    group_width = D // group_count
    left_shape = (N_SECTION, N_DP, TOK_DEV, group_count, RANK)
    right_shape = (N_SECTION, N_DP, group_count, RANK, group_width)
    noise_shape = (N_SECTION, N_DP, TOK_DEV, group_count, group_width)
    left = jax.random.normal(key_left, left_shape, jnp.float32)
    right = jax.random.normal(key_right, right_shape, jnp.float32)
    noise = jax.random.normal(key_noise, noise_shape, jnp.float32)
    right = right * RANK ** (-0.5)
    signal = jnp.einsum('sbtgr,sbgrw->sbtgw', left, right)
    whole = signal + 0.15 * noise
    return whole.reshape(N_SECTION, TOKENS, D)


def draw_section_output(key, part):
    return spectral_rows(jax.random.fold_in(key, 11)).astype(jnp.bfloat16)


def draw_grad_gained(key, part):
    return spectral_rows(jax.random.fold_in(key, 23)).astype(jnp.bfloat16)


def steps_of(rng, extent, cuts, low, high):
    gain, own = 1.0, jax.random.fold_in(rng, 6)
    for position, blocks in cuts:
        heights = jnp.exp(jax.random.uniform(jax.random.fold_in(own, position), (blocks,), jnp.float32, low / len(cuts), high / len(cuts)))
        gain = gain * jnp.repeat(heights, extent[position] // blocks).reshape([-1 if axis == position else 1 for axis in range(len(extent))])
    return gain


def gaussian(own_key, dims, width, most, pieces=(), kind=jnp.bfloat16):
    array = width * jax.random.normal(own_key, dims, jnp.float32)
    if pieces:
        array = array * steps_of(own_key, dims, pieces, -0.22, 0.18)
    return jnp.clip(array, -most, most).astype(kind)


def setup_inputs(seed: int = 0) -> dict:
    key_list = jax.random.split(jax.random.key(seed), 5)
    section_output = draw_section_output(jax.random.fold_in(key_list[4], 71), 0)
    sketch_matrix = gaussian(key_list[1], (N_SECTION, D, RANK), D ** -0.5, 0.046875, ((0, 32), (1, 4)))
    boundary_gain = jnp.clip(1.0 + 0.18 * jax.random.normal(key_list[2], (N_SECTION, D), jnp.float32), 0.099609375, 1.8984375).astype(jnp.bfloat16)
    grad_gained = draw_grad_gained(jax.random.fold_in(key_list[4], 71), 0)
    return {"section_output": section_output, "sketch_matrix": sketch_matrix, "boundary_gain": boundary_gain, "grad_gained": grad_gained}


def factorize(rows, sketch_cols):
    blocks = rows.reshape(N_DP, TOK_DEV, D).astype(jnp.float32)
    first = jnp.einsum('btd,dr->btr', blocks, sketch_cols.astype(jnp.float32)).astype(jnp.bfloat16)
    inner = jnp.einsum('btd,btr->bdr', blocks, first.astype(jnp.float32)).astype(jnp.bfloat16)
    sketch = jnp.einsum('btd,bdr->btr', blocks, inner.astype(jnp.float32))
    gram = jnp.einsum('btr,bts->brs', sketch, sketch, precision=lax.Precision.HIGHEST)
    ridge = 1e-06 * jnp.trace(gram, axis1=1, axis2=2) / RANK
    gram = gram + ridge[:, None, None] * jnp.eye(RANK, dtype=gram.dtype)[None]
    lower = jnp.linalg.cholesky(gram)
    basis = lax.linalg.triangular_solve(lower, sketch, left_side=False, lower=True, transpose_a=True).astype(jnp.bfloat16)
    coeff = jnp.einsum('btr,btd->brd', basis.astype(jnp.float32), blocks).astype(jnp.bfloat16)
    recon = jnp.einsum('btr,brd->btd', basis.astype(jnp.float32), coeff.astype(jnp.float32)).astype(jnp.bfloat16)
    return recon.reshape(TOKENS, D)

def reference(section_output, sketch_matrix, boundary_gain, grad_gained):
    forward_recon = lax.map(lambda pair: factorize(pair[0], pair[1]), (section_output, sketch_matrix))
    received = jnp.concatenate([jnp.zeros((1, TOKENS, D), jnp.bfloat16), forward_recon[:-1]], axis=0)
    gain_grad = jnp.sum(grad_gained.astype(jnp.float32) * received.astype(jnp.float32), axis=1)
    grad_received = (grad_gained.astype(jnp.float32) * boundary_gain.astype(jnp.float32)[:, None, :]).astype(jnp.bfloat16)
    backward_recon = lax.map(lambda pair: factorize(pair[0], pair[1]), (grad_received, sketch_matrix))
    grad_output = jnp.concatenate([backward_recon[1:], jnp.zeros((1, TOKENS, D), jnp.bfloat16)], axis=0)
    return (grad_output, gain_grad)
```

```python
import jax
import jax.numpy as jnp
from jax import lax
from jax.experimental import pallas as pl
from jax.experimental.pallas import tpu as pltpu
from jax.sharding import PartitionSpec as P


F32 = jnp.float32
BF16 = jnp.bfloat16
HIGHEST = lax.Precision.HIGHEST
RIDGE = 1e-06
SMALL = pltpu.CompilerParams(vmem_limit_bytes=16 * 1024 * 1024)
CONTRACT_LAST = (((1,), (1,)), ((), ()))
CONTRACT_FIRST = (((0,), (0,)), ((), ()))


def indices(shape):
    return (
        lax.broadcasted_iota(jnp.int32, shape, 0),
        lax.broadcasted_iota(jnp.int32, shape, 1),
    )


def packed(gram):
    half = gram.shape[0] // 2
    row, col = indices((half, 2 * half))
    turned = pltpu.roll(gram[half:], half, 1)
    return jnp.where((col < half) & (col >= row), turned, gram[:half])


def unpacked(rows, diagonal):
    half = rows.shape[0]
    row, col = indices((half, 2 * half))
    square = jnp.concatenate([rows, jnp.zeros_like(rows)], axis=0).T
    mirrored, below = square[:half], square[half:]
    first_half = jnp.where(row > col, rows, jnp.where(row < col, mirrored, diagonal))
    top = jnp.where(col < half, first_half, rows)
    shifted = col - half
    turned_rows = pltpu.roll(rows, half, 1)
    turned_mirrored = pltpu.roll(mirrored, half, 1)
    last_half = jnp.where(
        row < shifted, turned_rows, jnp.where(row > shifted, turned_mirrored, diagonal)
    )
    bottom = jnp.where(col < half, below, last_half)
    return jnp.concatenate([top, bottom], axis=0)


def partials_kernel(rows_ref, grad_ref, gain_ref, sketch_ref, out_ref, forward_acc, backward_acc):
    step = pl.program_id(0)
    tokens = rows_ref.shape[0]
    sketch = sketch_ref[...]
    rows = rows_ref[...]
    gained = (grad_ref[...].astype(F32) * gain_ref[...].astype(F32)).astype(BF16)

    def products(block):
        both = jnp.concatenate([block, sketch], axis=0)
        return lax.dot_general(both, block, CONTRACT_LAST, preferred_element_type=F32)

    forward = products(rows)
    backward = products(gained)

    @pl.when(step == 0)
    def _():
        forward_acc[...] = forward
        backward_acc[...] = backward

    @pl.when(step > 0)
    def _():
        forward_acc[...] += forward
        backward_acc[...] += backward

    @pl.when(step == pl.num_programs(0) - 1)
    def _():
        half = tokens // 2
        rank = sketch.shape[0]
        row, col = indices((tokens, tokens))
        diagonals = []
        for turn, acc in enumerate((forward_acc, backward_acc)):
            gram = acc[:tokens]
            out_ref[turn * half : (turn + 1) * half] = packed(gram).astype(BF16)
            at = 2 * half + turn * rank
            out_ref[at : at + rank] = acc[tokens:].astype(BF16)
            diagonal = jnp.sum(jnp.where(row == col, gram, 0.0), axis=0, keepdims=True)
            high = diagonal.astype(BF16).astype(F32)
            diagonals += [high, diagonal - high]
        rest = jnp.zeros((out_ref.shape[0] - 2 * half - 2 * rank - 4, tokens), F32)
        tail = jnp.concatenate(diagonals + [rest], axis=0)
        out_ref[2 * half + 2 * rank :] = tail.astype(BF16)


def orthonormal(gram, first):
    rank, _ = first.shape
    sketch = lax.dot_general(
        first, gram, (((1,), (0,)), ((), ())), precision=HIGHEST, preferred_element_type=F32
    )
    small = lax.dot_general(
        sketch, sketch, CONTRACT_LAST, precision=HIGHEST, preferred_element_type=F32
    )
    row, col = indices((rank, rank))
    trace = jnp.sum(jnp.where(row == col, small, 0.0), keepdims=True)
    small = small + jnp.where(row == col, trace * (RIDGE / rank), 0.0)
    return sketch, small


def eliminate(pairs):
    rank = pairs[0][0].shape[0]
    states = [list(pair) for pair in pairs]
    done = [[] for _ in pairs]
    for k in range(rank):
        for state, finished in zip(states, done):
            sketch, small = state
            pivot = small[k : k + 1, k : k + 1]
            scale = lax.rsqrt(pivot)
            scale = scale * (1.5 - 0.5 * pivot * scale * scale)
            sketch_row = sketch[k : k + 1] * scale
            finished.append(sketch_row)
            if k + 1 < rank:
                small_row = small[k : k + 1] * scale
                column = small[:, k : k + 1] * scale
                state[0] = sketch - column * sketch_row
                state[1] = small - column * small_row
    return [jnp.concatenate(finished, axis=0) for finished in done]


def factor_kernel(
    gathered_ref, rows_hbm, next_hbm, local_ref, forward_ref, backward_ref, rows_ref, next_ref, sems
):
    copies = [
        pltpu.make_async_copy(rows_hbm, rows_ref, sems.at[0]),
        pltpu.make_async_copy(next_hbm, next_ref, sems.at[1]),
    ]
    for copy in copies:
        copy.start()
    tokens, width = rows_ref.shape
    rank = backward_ref.shape[0]
    half = tokens // 2
    total = gathered_ref[0].astype(F32)
    for member in range(1, gathered_ref.shape[0]):
        total = total + gathered_ref[member].astype(F32)
    pairs = []
    for turn in range(2):
        at = 2 * half + turn * rank
        mark = 2 * half + 2 * rank + 2 * turn
        diagonal = total[mark : mark + 1] + total[mark + 1 : mark + 2]
        gram = unpacked(total[turn * half : (turn + 1) * half], diagonal)
        pairs.append(orthonormal(gram, total[at : at + rank]))
    forward, backward = (basis.astype(BF16) for basis in eliminate(pairs))
    forward_ref[...] = forward
    backward_ref[...] = backward
    for copy in copies:
        copy.wait()
    chunk = 1024
    for start in range(0, width, chunk):
        coeff = jnp.dot(
            forward, rows_ref[:, start : start + chunk], preferred_element_type=F32
        ).astype(BF16)
        other = jnp.dot(forward, next_ref[:, start : start + chunk], preferred_element_type=F32)
        summed = jnp.sum(coeff.astype(F32) * other, axis=0, keepdims=True)
        for lane in range(0, chunk, 128):
            at = (start + lane) // 128
            local_ref[at : at + 1] = summed[:, lane : lane + 128]


def coeff_kernel(basis_ref, grad_ref, gain_ref, out_ref):
    width = grad_ref.shape[1]
    basis = basis_ref[...]
    gained = (grad_ref[...].astype(F32) * gain_ref[...].astype(F32)).astype(BF16)
    out_ref[:, :width] = jnp.dot(basis, gained, preferred_element_type=F32).astype(BF16)
    out_ref[:, width:] = basis


def rebuild_kernel(coeff_ref, basis_ref, out_ref):
    out_ref[...] = lax.dot_general(
        basis_ref[...], coeff_ref[...], CONTRACT_FIRST, preferred_element_type=F32
    ).astype(BF16)


def partials(rows, grad, gain, sketch_rows):
    tokens, width = rows.shape
    rank = sketch_rows.shape[0]
    chunk = 1024
    return pl.pallas_call(
        partials_kernel,
        out_shape=jax.ShapeDtypeStruct((tokens + 2 * rank + 8, tokens), BF16),
        grid=(width // chunk,),
        in_specs=[
            pl.BlockSpec((tokens, chunk), lambda i: (0, i)),
            pl.BlockSpec((tokens, chunk), lambda i: (0, i)),
            pl.BlockSpec((1, chunk), lambda i: (0, i)),
            pl.BlockSpec((rank, chunk), lambda i: (0, i)),
        ],
        out_specs=pl.BlockSpec((tokens + 2 * rank + 8, tokens), lambda i: (0, 0)),
        scratch_shapes=[
            pltpu.VMEM((tokens + rank, tokens), F32),
            pltpu.VMEM((tokens + rank, tokens), F32),
        ],
        name="partials",
    )(rows, grad, gain, sketch_rows)


def factors(gathered, rows, next_grad, rank):
    tokens, width = rows.shape
    vmem = pl.BlockSpec(memory_space=pltpu.VMEM)
    anywhere = pl.BlockSpec(memory_space=pl.ANY)
    basis = jax.ShapeDtypeStruct((rank, tokens), BF16)
    return pl.pallas_call(
        factor_kernel,
        out_shape=(jax.ShapeDtypeStruct((width // 128, 128), F32), basis, basis),
        in_specs=[vmem, anywhere, anywhere],
        out_specs=(vmem, vmem, vmem),
        scratch_shapes=[
            pltpu.VMEM((tokens, width), BF16),
            pltpu.VMEM((tokens, width), BF16),
            pltpu.SemaphoreType.DMA((2,)),
        ],
        compiler_params=SMALL,
        name="factors",
    )(gathered, rows, next_grad)


def coefficients(basis, grad, gain):
    rank, tokens = basis.shape
    width = grad.shape[1]
    vmem = pl.BlockSpec(memory_space=pltpu.VMEM)
    return pl.pallas_call(
        coeff_kernel,
        out_shape=jax.ShapeDtypeStruct((rank, width + tokens), BF16),
        in_specs=[vmem, vmem, vmem],
        out_specs=vmem,
        compiler_params=SMALL,
        name="coefficients",
    )(basis, grad, gain)


def rebuild(both, tokens):
    rank = both.shape[0]
    width = both.shape[1] - tokens
    chunk = 1024
    return pl.pallas_call(
        rebuild_kernel,
        out_shape=jax.ShapeDtypeStruct((tokens, width), BF16),
        grid=(width // chunk,),
        in_specs=[
            pl.BlockSpec((rank, chunk), lambda i: (0, i)),
            pl.BlockSpec((rank, tokens), lambda i: (0, width // tokens)),
        ],
        out_specs=pl.BlockSpec((tokens, chunk), lambda i: (0, i)),
        compiler_params=SMALL,
        name="rebuild",
    )(both, both)


def along_section(block, distance):
    devices = range(lax.axis_size("section"))
    route = [(i, i + distance) for i in devices if i + distance in devices]
    return lax.ppermute(block, "section", route)


def exchange(block, bit):
    return lax.ppermute(block, "dp", [(i, i ^ bit) for i in range(lax.axis_size("dp"))])


def exchange_along(block, bit):
    sections, members = lax.axis_size("section"), lax.axis_size("dp")
    route = [
        (i * sections + s, (i ^ bit) * sections + s + 1)
        for i in range(members)
        for s in range(sections - 1)
    ]
    return lax.ppermute(block, ("dp", "section"), route)


def shards(section_output, sketch_matrix, boundary_gain, grad_gained):
    rows = section_output[0]
    sketch_rows = sketch_matrix[0].T
    grad = grad_gained[0]
    tokens = rows.shape[0]
    next_grad = along_section(grad, -1)
    mine = partials(rows, grad, boundary_gain, sketch_rows)
    gathered = lax.all_gather(mine, "tensor")
    local, _, backward = factors(gathered, rows, next_grad, sketch_rows.shape[0])
    far = exchange(local, 4)
    both = coefficients(backward, grad, boundary_gain)
    both = along_section(both, -1)
    summed = local + far
    middle = exchange(summed, 2)
    summed = summed + middle
    own = exchange_along(summed, 0)
    near = exchange_along(summed, 1)
    gain_grad = own + near
    grad_output = rebuild(both, tokens)
    return grad_output[None], gain_grad.reshape(1, -1)


def solution(mesh):
    return jax.shard_map(
        shards,
        mesh=mesh,
        in_specs=(
            P("section", "dp", "tensor"),
            P("section", "tensor", None),
            P("section", "tensor"),
            P("section", "dp", "tensor"),
        ),
        out_specs=(P("section", "dp", "tensor"), P("section", "tensor")),
        check_vma=False,
    )
```

```python
import jax
import jax.numpy as jnp
from jax import lax
from jax.experimental import pallas as pl
from jax.experimental.pallas import tpu as pltpu
from jax.sharding import PartitionSpec as P


F32 = jnp.float32
BF16 = jnp.bfloat16
HIGHEST = lax.Precision.HIGHEST
RIDGE = 1e-06
CHUNKS = 4
BLOCK = 4
SMALL = pltpu.CompilerParams(vmem_limit_bytes=16 * 1024 * 1024)
CONTRACT_LAST = (((1,), (1,)), ((), ()))


def indices(shape):
    return (
        lax.broadcasted_iota(jnp.int32, shape, 0),
        lax.broadcasted_iota(jnp.int32, shape, 1),
    )


def packed(gram):
    half = gram.shape[0] // 2
    row, col = indices((half, 2 * half))
    turned = pltpu.roll(gram[half:], half, 1)
    return jnp.where((col < half) & (col >= row), turned, gram[:half])


def unpacked(rows, diagonal):
    half = rows.shape[0]
    row, col = indices((half, 2 * half))
    square = jnp.concatenate([rows, jnp.zeros_like(rows)], axis=0).T
    mirrored, below = square[:half], square[half:]
    first_half = jnp.where(row > col, rows, jnp.where(row < col, mirrored, diagonal))
    top = jnp.where(col < half, first_half, rows)
    shifted = col - half
    turned_rows = pltpu.roll(rows, half, 1)
    turned_mirrored = pltpu.roll(mirrored, half, 1)
    last_half = jnp.where(
        row < shifted, turned_rows, jnp.where(row > shifted, turned_mirrored, diagonal)
    )
    bottom = jnp.where(col < half, below, last_half)
    return jnp.concatenate([top, bottom], axis=0)


def partials_kernel(
    rows_hbm, grad_hbm, gain_hbm, sketch_hbm, out_ref, rows_ref, grad_ref, gain_ref, sketch_ref, sems
):
    tokens, width = rows_ref.shape
    rank = sketch_ref.shape[0]
    chunk = width // CHUNKS
    small = [
        pltpu.make_async_copy(sketch_hbm, sketch_ref, sems.at[2 * CHUNKS]),
        pltpu.make_async_copy(gain_hbm, gain_ref, sems.at[2 * CHUNKS + 1]),
    ]
    large = []
    for turn, (source, target) in enumerate(((rows_hbm, rows_ref), (grad_hbm, grad_ref))):
        for i in range(CHUNKS):
            at = pl.ds(i * chunk, chunk)
            large.append(
                pltpu.make_async_copy(
                    source.at[:, at], target.at[:, at], sems.at[turn * CHUNKS + i]
                )
            )
    for copy in small + large:
        copy.start()
    for copy in small:
        copy.wait()
    totals = []
    for turn in range(2):
        total = None
        for i in range(CHUNKS):
            at = slice(i * chunk, (i + 1) * chunk)
            large[turn * CHUNKS + i].wait()
            if turn == 0:
                block = rows_ref[:, at]
            else:
                block = grad_ref[:, at].astype(F32) * gain_ref[:, at].astype(F32)
                block = block.astype(BF16)
            product = [
                lax.dot_general(left, block, CONTRACT_LAST, preferred_element_type=F32)
                for left in (block, sketch_ref[:, at])
            ]
            total = product if total is None else [a + b for a, b in zip(total, product)]
        totals.append(total)
    half = tokens // 2
    row, col = indices((tokens, tokens))
    diagonals = []
    for turn, (gram, first) in enumerate(totals):
        out_ref[turn * half : (turn + 1) * half] = packed(gram).astype(BF16)
        at = 2 * half + turn * rank
        out_ref[at : at + rank] = first.astype(BF16)
        diagonal = jnp.sum(jnp.where(row == col, gram, 0.0), axis=0, keepdims=True)
        high = diagonal.astype(BF16).astype(F32)
        diagonals += [high, diagonal - high]
    rest = jnp.zeros((out_ref.shape[0] - 2 * half - 2 * rank - 4, tokens), F32)
    tail = jnp.concatenate(diagonals + [rest], axis=0)
    out_ref[2 * half + 2 * rank :] = tail.astype(BF16)


def orthonormal(gram, first):
    rank, _ = first.shape
    sketch = lax.dot_general(
        first, gram, (((1,), (0,)), ((), ())), precision=HIGHEST, preferred_element_type=F32
    )
    small = lax.dot_general(
        sketch, sketch, CONTRACT_LAST, precision=HIGHEST, preferred_element_type=F32
    )
    row, col = indices((rank, rank))
    trace = jnp.sum(jnp.where(row == col, small, 0.0), keepdims=True)
    small = small + jnp.where(row == col, trace * (RIDGE / rank), 0.0)
    return sketch, small


def eliminate(pairs):
    rank, tokens = pairs[0][0].shape
    states = [
        jnp.concatenate(
            [sketch, small, jnp.zeros((rank, tokens - rank), F32)], axis=1
        )
        for sketch, small in pairs
    ]
    done = [[] for _ in pairs]
    for start in range(0, rank, BLOCK):
        spread = [
            [
                jnp.broadcast_to(
                    state[:, tokens + k : tokens + k + 1], (rank, tokens)
                )
                for k in range(start, start + BLOCK)
            ]
            for state in states
        ]
        for j in range(BLOCK):
            k = start + j
            for n, columns in enumerate(spread):
                column = columns[j]
                pivot = column[k : k + 1]
                inverse = 1.0 / pivot
                inverse2 = jnp.concatenate([inverse, inverse], axis=1)
                row = states[n][k : k + 1]
                scale = lax.rsqrt(pivot)
                scale = scale * (1.5 - 0.5 * pivot * scale * scale)
                done[n].append(row[:, :tokens] * scale)
                column2 = jnp.concatenate([column, column], axis=1)
                states[n] = states[n] - column2 * (row * inverse2)
                for m in range(j + 1, BLOCK):
                    other = column[start + m : start + m + 1] * inverse
                    columns[m] = columns[m] - column * other
    return [jnp.concatenate(finished, axis=0) for finished in done]


def factor_kernel(
    gathered_ref, rows_hbm, next_hbm, local_ref, forward_ref, backward_ref, rows_ref, next_ref, sems
):
    copies = [
        pltpu.make_async_copy(rows_hbm, rows_ref, sems.at[0]),
        pltpu.make_async_copy(next_hbm, next_ref, sems.at[1]),
    ]
    for copy in copies:
        copy.start()
    tokens, width = rows_ref.shape
    rank = backward_ref.shape[0]
    half = tokens // 2
    total = gathered_ref[0].astype(F32)
    for member in range(1, gathered_ref.shape[0]):
        total = total + gathered_ref[member].astype(F32)
    pairs = []
    for turn in range(2):
        at = 2 * half + turn * rank
        mark = 2 * half + 2 * rank + 2 * turn
        diagonal = total[mark : mark + 1] + total[mark + 1 : mark + 2]
        gram = unpacked(total[turn * half : (turn + 1) * half], diagonal)
        pairs.append(orthonormal(gram, total[at : at + rank]))
    forward, backward = (basis.astype(BF16) for basis in eliminate(pairs))
    forward_ref[...] = forward
    backward_ref[...] = backward
    for copy in copies:
        copy.wait()
    chunk = 1024
    for start in range(0, width, chunk):
        coeff = jnp.dot(
            forward, rows_ref[:, start : start + chunk], preferred_element_type=F32
        ).astype(BF16)
        other = jnp.dot(forward, next_ref[:, start : start + chunk], preferred_element_type=F32)
        summed = jnp.sum(coeff.astype(F32) * other, axis=0, keepdims=True)
        for lane in range(0, chunk, 128):
            at = (start + lane) // 128
            local_ref[at : at + 1] = summed[:, lane : lane + 128]


def coeff_kernel(basis_ref, grad_ref, gain_ref, out_ref):
    width = grad_ref.shape[1]
    basis = basis_ref[...]
    gained = (grad_ref[...].astype(F32) * gain_ref[...].astype(F32)).astype(BF16)
    out_ref[:, :width] = jnp.dot(basis, gained, preferred_element_type=F32).astype(BF16)
    out_ref[:, width:] = basis


def rebuild_kernel(both_ref, out_hbm, out_ref, sems):
    _, width = out_ref.shape
    basis = both_ref[:, width:].T
    chunk = width // CHUNKS
    copies = []
    for i in range(CHUNKS):
        at = i * chunk
        out_ref[:, at : at + chunk] = jnp.dot(
            basis, both_ref[:, at : at + chunk], preferred_element_type=F32
        ).astype(BF16)
        window = pl.ds(at, chunk)
        copies.append(
            pltpu.make_async_copy(out_ref.at[:, window], out_hbm.at[:, window], sems.at[i])
        )
        copies[-1].start()
    for copy in copies:
        copy.wait()


def partials(rows, grad, gain, sketch_rows):
    tokens, width = rows.shape
    rank = sketch_rows.shape[0]
    anywhere = pl.BlockSpec(memory_space=pl.ANY)
    return pl.pallas_call(
        partials_kernel,
        out_shape=jax.ShapeDtypeStruct((tokens + 2 * rank + 8, tokens), BF16),
        in_specs=[anywhere] * 4,
        out_specs=pl.BlockSpec(memory_space=pltpu.VMEM),
        scratch_shapes=[
            pltpu.VMEM((tokens, width), BF16),
            pltpu.VMEM((tokens, width), BF16),
            pltpu.VMEM((1, width), BF16),
            pltpu.VMEM((rank, width), BF16),
            pltpu.SemaphoreType.DMA((2 * CHUNKS + 2,)),
        ],
        name="partials",
    )(rows, grad, gain, sketch_rows)


def factors(gathered, rows, next_grad, rank):
    tokens, width = rows.shape
    vmem = pl.BlockSpec(memory_space=pltpu.VMEM)
    anywhere = pl.BlockSpec(memory_space=pl.ANY)
    basis = jax.ShapeDtypeStruct((rank, tokens), BF16)
    return pl.pallas_call(
        factor_kernel,
        out_shape=(jax.ShapeDtypeStruct((width // 128, 128), F32), basis, basis),
        in_specs=[vmem, anywhere, anywhere],
        out_specs=(vmem, vmem, vmem),
        scratch_shapes=[
            pltpu.VMEM((tokens, width), BF16),
            pltpu.VMEM((tokens, width), BF16),
            pltpu.SemaphoreType.DMA((2,)),
        ],
        compiler_params=SMALL,
        name="factors",
    )(gathered, rows, next_grad)


def coefficients(basis, grad, gain):
    rank, tokens = basis.shape
    width = grad.shape[1]
    vmem = pl.BlockSpec(memory_space=pltpu.VMEM)
    return pl.pallas_call(
        coeff_kernel,
        out_shape=jax.ShapeDtypeStruct((rank, width + tokens), BF16),
        in_specs=[vmem, vmem, vmem],
        out_specs=vmem,
        compiler_params=SMALL,
        name="coefficients",
    )(basis, grad, gain)


def rebuild(both, tokens):
    width = both.shape[1] - tokens
    return pl.pallas_call(
        rebuild_kernel,
        out_shape=jax.ShapeDtypeStruct((tokens, width), BF16),
        in_specs=[pl.BlockSpec(memory_space=pltpu.VMEM)],
        out_specs=pl.BlockSpec(memory_space=pl.ANY),
        scratch_shapes=[
            pltpu.VMEM((tokens, width), BF16),
            pltpu.SemaphoreType.DMA((CHUNKS,)),
        ],
        compiler_params=SMALL,
        name="rebuild",
    )(both)


def along_section(block, distance):
    devices = range(lax.axis_size("section"))
    route = [(i, i + distance) for i in devices if i + distance in devices]
    return lax.ppermute(block, "section", route)


def exchange(block, bit):
    return lax.ppermute(block, "dp", [(i, i ^ bit) for i in range(lax.axis_size("dp"))])


def exchange_along(block, bit):
    sections, members = lax.axis_size("section"), lax.axis_size("dp")
    route = [
        (i * sections + s, (i ^ bit) * sections + s + 1)
        for i in range(members)
        for s in range(sections - 1)
    ]
    return lax.ppermute(block, ("dp", "section"), route)


def shards(section_output, sketch_matrix, boundary_gain, grad_gained):
    rows = section_output[0]
    sketch_rows = sketch_matrix[0].T
    grad = grad_gained[0]
    tokens = rows.shape[0]
    next_grad = along_section(grad, -1)
    mine = partials(rows, grad, boundary_gain, sketch_rows)
    gathered = lax.all_gather(mine, "tensor")
    local, _, backward = factors(gathered, rows, next_grad, sketch_rows.shape[0])
    far = exchange(local, 4)
    both = coefficients(backward, grad, boundary_gain)
    both = along_section(both, -1)
    summed = local + far
    middle = exchange(summed, 2)
    summed = summed + middle
    own = exchange_along(summed, 0)
    near = exchange_along(summed, 1)
    gain_grad = own + near
    grad_output = rebuild(both, tokens)
    return grad_output[None], gain_grad.reshape(1, -1)


def solution(mesh):
    return jax.shard_map(
        shards,
        mesh=mesh,
        in_specs=(
            P("section", "dp", "tensor"),
            P("section", "tensor", None),
            P("section", "tensor"),
            P("section", "dp", "tensor"),
        ),
        out_specs=(P("section", "dp", "tensor"), P("section", "tensor")),
        check_vma=False,
    )
```

```python
import jax
import jax.numpy as jnp
from jax import lax
from jax.experimental import pallas as pl
from jax.experimental.pallas import tpu as pltpu
from jax.sharding import PartitionSpec as P


F32 = jnp.float32
BF16 = jnp.bfloat16
HIGHEST = lax.Precision.HIGHEST
RIDGE = 1e-06
CHUNKS = 4
BLOCK = 4
SMALL = pltpu.CompilerParams(vmem_limit_bytes=16 * 1024 * 1024)
CONTRACT_LAST = (((1,), (1,)), ((), ()))


def indices(shape):
    return (
        lax.broadcasted_iota(jnp.int32, shape, 0),
        lax.broadcasted_iota(jnp.int32, shape, 1),
    )


def packed(gram):
    half = gram.shape[0] // 2
    row, col = indices((half, 2 * half))
    turned = pltpu.roll(gram[half:], half, 1)
    return jnp.where((col < half) & (col >= row), turned, gram[:half])


def unpacked(rows, diagonal):
    half = rows.shape[0]
    row, col = indices((half, 2 * half))
    square = jnp.concatenate([rows, jnp.zeros_like(rows)], axis=0).T
    mirrored, below = square[:half], square[half:]
    first_half = jnp.where(row > col, rows, jnp.where(row < col, mirrored, diagonal))
    top = jnp.where(col < half, first_half, rows)
    shifted = col - half
    turned_rows = pltpu.roll(rows, half, 1)
    turned_mirrored = pltpu.roll(mirrored, half, 1)
    last_half = jnp.where(
        row < shifted, turned_rows, jnp.where(row > shifted, turned_mirrored, diagonal)
    )
    bottom = jnp.where(col < half, below, last_half)
    return jnp.concatenate([top, bottom], axis=0)


def partials_kernel(
    rows_hbm, grad_hbm, gain_hbm, sketch_hbm, out_ref, rows_ref, grad_ref, gain_ref, sketch_ref, sems
):
    tokens, width = rows_ref.shape
    rank = sketch_ref.shape[0]
    chunk = width // CHUNKS
    small = [
        pltpu.make_async_copy(sketch_hbm, sketch_ref, sems.at[2 * CHUNKS]),
        pltpu.make_async_copy(gain_hbm, gain_ref, sems.at[2 * CHUNKS + 1]),
    ]
    large = []
    for turn, (source, target) in enumerate(((rows_hbm, rows_ref), (grad_hbm, grad_ref))):
        for i in range(CHUNKS):
            at = pl.ds(i * chunk, chunk)
            large.append(
                pltpu.make_async_copy(
                    source.at[:, at], target.at[:, at], sems.at[turn * CHUNKS + i]
                )
            )
    for copy in small + large:
        copy.start()
    for copy in small:
        copy.wait()
    totals = []
    for turn in range(2):
        total = None
        for i in range(CHUNKS):
            at = slice(i * chunk, (i + 1) * chunk)
            large[turn * CHUNKS + i].wait()
            if turn == 0:
                block = rows_ref[:, at]
            else:
                block = grad_ref[:, at].astype(F32) * gain_ref[:, at].astype(F32)
                block = block.astype(BF16)
            product = [
                lax.dot_general(left, block, CONTRACT_LAST, preferred_element_type=F32)
                for left in (block, sketch_ref[:, at])
            ]
            total = product if total is None else [a + b for a, b in zip(total, product)]
        totals.append(total)
    half = tokens // 2
    row, col = indices((tokens, tokens))
    diagonals = []
    for turn, (gram, first) in enumerate(totals):
        out_ref[turn * half : (turn + 1) * half] = packed(gram).astype(BF16)
        at = 2 * half + turn * rank
        out_ref[at : at + rank] = first.astype(BF16)
        diagonal = jnp.sum(jnp.where(row == col, gram, 0.0), axis=0, keepdims=True)
        high = diagonal.astype(BF16).astype(F32)
        diagonals += [high, diagonal - high]
    rest = jnp.zeros((out_ref.shape[0] - 2 * half - 2 * rank - 4, tokens), F32)
    tail = jnp.concatenate(diagonals + [rest], axis=0)
    out_ref[2 * half + 2 * rank :] = tail.astype(BF16)


def orthonormal(gram, first):
    rank, _ = first.shape
    sketch = lax.dot_general(
        first, gram, (((1,), (0,)), ((), ())), precision=HIGHEST, preferred_element_type=F32
    )
    small = lax.dot_general(
        sketch, sketch, CONTRACT_LAST, precision=HIGHEST, preferred_element_type=F32
    )
    row, col = indices((rank, rank))
    trace = jnp.sum(jnp.where(row == col, small, 0.0), keepdims=True)
    small = small + jnp.where(row == col, trace * (RIDGE / rank), 0.0)
    return sketch, small


def eliminate(pairs):
    rank, tokens = pairs[0][0].shape
    states = [
        jnp.concatenate(
            [sketch, small, jnp.zeros((rank, tokens - rank), F32)], axis=1
        )
        for sketch, small in pairs
    ]
    done = [[] for _ in pairs]
    for start in range(0, rank, BLOCK):
        spread = [
            [
                jnp.broadcast_to(
                    state[:, tokens + k : tokens + k + 1], (rank, tokens)
                )
                for k in range(start, start + BLOCK)
            ]
            for state in states
        ]
        for j in range(BLOCK):
            k = start + j
            for n, columns in enumerate(spread):
                column = columns[j]
                pivot = column[k : k + 1]
                inverse = 1.0 / pivot
                inverse2 = jnp.concatenate([inverse, inverse], axis=1)
                row = states[n][k : k + 1]
                scale = lax.rsqrt(pivot)
                scale = scale * (1.5 - 0.5 * pivot * scale * scale)
                done[n].append(row[:, :tokens] * scale)
                column2 = jnp.concatenate([column, column], axis=1)
                states[n] = states[n] - column2 * (row * inverse2)
                for m in range(j + 1, BLOCK):
                    other = column[start + m : start + m + 1] * inverse
                    columns[m] = columns[m] - column * other
    return [jnp.concatenate(finished, axis=0) for finished in done]


def factor_kernel(
    gathered_ref, rows_hbm, next_hbm, spread_ref, backward_ref, local_ref, rows_ref, next_ref, sems
):
    copies = [
        pltpu.make_async_copy(rows_hbm, rows_ref, sems.at[0]),
        pltpu.make_async_copy(next_hbm, next_ref, sems.at[1]),
    ]
    for copy in copies:
        copy.start()
    tokens, width = rows_ref.shape
    rank = backward_ref.shape[0]
    half = tokens // 2
    total = gathered_ref[0].astype(F32)
    for member in range(1, gathered_ref.shape[0]):
        total = total + gathered_ref[member].astype(F32)
    pairs = []
    for turn in range(2):
        at = 2 * half + turn * rank
        mark = 2 * half + 2 * rank + 2 * turn
        diagonal = total[mark : mark + 1] + total[mark + 1 : mark + 2]
        gram = unpacked(total[turn * half : (turn + 1) * half], diagonal)
        pairs.append(orthonormal(gram, total[at : at + rank]))
    forward, backward = (basis.astype(BF16) for basis in eliminate(pairs))
    backward_ref[...] = backward
    for copy in copies:
        copy.wait()
    chunk = 1024
    for start in range(0, width, chunk):
        coeff = jnp.dot(
            forward, rows_ref[:, start : start + chunk], preferred_element_type=F32
        ).astype(BF16)
        other = jnp.dot(forward, next_ref[:, start : start + chunk], preferred_element_type=F32)
        summed = jnp.sum(coeff.astype(F32) * other, axis=0, keepdims=True)
        for lane in range(0, chunk, 128):
            at = (start + lane) // 128
            local_ref[at : at + 1] = summed[:, lane : lane + 128]
    local = local_ref[...].astype(BF16)
    for i in range(spread_ref.shape[0]):
        spread_ref[i] = local


def coeff_kernel(basis_ref, grad_ref, gain_ref, out_ref):
    width = grad_ref.shape[1]
    basis = basis_ref[...]
    gained = (grad_ref[...].astype(F32) * gain_ref[...].astype(F32)).astype(BF16)
    out_ref[:, :width] = jnp.dot(basis, gained, preferred_element_type=F32).astype(BF16)
    out_ref[:, width:] = basis


def rebuild_kernel(both_ref, out_hbm, out_ref, sems):
    _, width = out_ref.shape
    basis = both_ref[:, width:].T
    chunk = width // CHUNKS
    copies = []
    for i in range(CHUNKS):
        at = i * chunk
        out_ref[:, at : at + chunk] = jnp.dot(
            basis, both_ref[:, at : at + chunk], preferred_element_type=F32
        ).astype(BF16)
        window = pl.ds(at, chunk)
        copies.append(
            pltpu.make_async_copy(out_ref.at[:, window], out_hbm.at[:, window], sems.at[i])
        )
        copies[-1].start()
    for copy in copies:
        copy.wait()


def partials(rows, grad, gain, sketch_rows):
    tokens, width = rows.shape
    rank = sketch_rows.shape[0]
    anywhere = pl.BlockSpec(memory_space=pl.ANY)
    return pl.pallas_call(
        partials_kernel,
        out_shape=jax.ShapeDtypeStruct((tokens + 2 * rank + 8, tokens), BF16),
        in_specs=[anywhere] * 4,
        out_specs=pl.BlockSpec(memory_space=pltpu.VMEM),
        scratch_shapes=[
            pltpu.VMEM((tokens, width), BF16),
            pltpu.VMEM((tokens, width), BF16),
            pltpu.VMEM((1, width), BF16),
            pltpu.VMEM((rank, width), BF16),
            pltpu.SemaphoreType.DMA((2 * CHUNKS + 2,)),
        ],
        name="partials",
    )(rows, grad, gain, sketch_rows)


def factors(gathered, rows, next_grad, rank, copies):
    tokens, width = rows.shape
    vmem = pl.BlockSpec(memory_space=pltpu.VMEM)
    anywhere = pl.BlockSpec(memory_space=pl.ANY)
    basis = jax.ShapeDtypeStruct((rank, tokens), BF16)
    return pl.pallas_call(
        factor_kernel,
        out_shape=(jax.ShapeDtypeStruct((copies, width // 128, 128), BF16), basis),
        in_specs=[vmem, anywhere, anywhere],
        out_specs=(vmem, vmem),
        scratch_shapes=[
            pltpu.VMEM((width // 128, 128), F32),
            pltpu.VMEM((tokens, width), BF16),
            pltpu.VMEM((tokens, width), BF16),
            pltpu.SemaphoreType.DMA((2,)),
        ],
        compiler_params=SMALL,
        name="factors",
    )(gathered, rows, next_grad)


def coefficients(basis, grad, gain):
    rank, tokens = basis.shape
    width = grad.shape[1]
    vmem = pl.BlockSpec(memory_space=pltpu.VMEM)
    return pl.pallas_call(
        coeff_kernel,
        out_shape=jax.ShapeDtypeStruct((rank, width + tokens), BF16),
        in_specs=[vmem, vmem, vmem],
        out_specs=vmem,
        compiler_params=SMALL,
        name="coefficients",
    )(basis, grad, gain)


def rebuild(both, tokens):
    width = both.shape[1] - tokens
    return pl.pallas_call(
        rebuild_kernel,
        out_shape=jax.ShapeDtypeStruct((tokens, width), BF16),
        in_specs=[pl.BlockSpec(memory_space=pltpu.VMEM)],
        out_specs=pl.BlockSpec(memory_space=pl.ANY),
        scratch_shapes=[
            pltpu.VMEM((tokens, width), BF16),
            pltpu.SemaphoreType.DMA((CHUNKS,)),
        ],
        compiler_params=SMALL,
        name="rebuild",
    )(both)


def along_section(block, distance):
    devices = range(lax.axis_size("section"))
    route = [(i, i + distance) for i in devices if i + distance in devices]
    return lax.ppermute(block, "section", route)


def shards(section_output, sketch_matrix, boundary_gain, grad_gained):
    rows = section_output[0]
    sketch_rows = sketch_matrix[0].T
    grad = grad_gained[0]
    tokens = rows.shape[0]
    next_grad = along_section(grad, -1)
    mine = partials(rows, grad, boundary_gain, sketch_rows)
    gathered = lax.all_gather(mine, "tensor")
    local, backward = factors(gathered, rows, next_grad, sketch_rows.shape[0], lax.axis_size("dp"))
    both = coefficients(backward, grad, boundary_gain)
    both = along_section(both, -1)
    locals_ = lax.all_to_all(local, "dp", 0, 0)
    summed = jnp.sum(locals_.astype(F32), axis=0)
    gain_grad = along_section(summed, 1)
    grad_output = rebuild(both, tokens)
    return grad_output[None], gain_grad.reshape(1, -1)


def solution(mesh):
    return jax.shard_map(
        shards,
        mesh=mesh,
        in_specs=(
            P("section", "dp", "tensor"),
            P("section", "tensor", None),
            P("section", "tensor"),
            P("section", "dp", "tensor"),
        ),
        out_specs=(P("section", "dp", "tensor"), P("section", "tensor")),
        check_vma=False,
    )
```

```python
import jax
import jax.numpy as jnp
from jax import lax
from jax.experimental import pallas as pl
from jax.experimental.pallas import tpu as pltpu
from jax.sharding import PartitionSpec as P


F32 = jnp.float32
BF16 = jnp.bfloat16
HIGHEST = lax.Precision.HIGHEST
RIDGE = 1e-06
CHUNKS = 4
BLOCK = 4
SMALL = pltpu.CompilerParams(vmem_limit_bytes=16 * 1024 * 1024)
CONTRACT_LAST = (((1,), (1,)), ((), ()))


def indices(shape):
    return (
        lax.broadcasted_iota(jnp.int32, shape, 0),
        lax.broadcasted_iota(jnp.int32, shape, 1),
    )


def packed(gram):
    half = gram.shape[0] // 2
    row, col = indices((half, 2 * half))
    turned = pltpu.roll(gram[half:], half, 1)
    return jnp.where((col < half) & (col >= row), turned, gram[:half])


def unpacked(rows, diagonal):
    half = rows.shape[0]
    row, col = indices((half, 2 * half))
    square = jnp.concatenate([rows, jnp.zeros_like(rows)], axis=0).T
    mirrored, below = square[:half], square[half:]
    first_half = jnp.where(row > col, rows, jnp.where(row < col, mirrored, diagonal))
    top = jnp.where(col < half, first_half, rows)
    shifted = col - half
    turned_rows = pltpu.roll(rows, half, 1)
    turned_mirrored = pltpu.roll(mirrored, half, 1)
    last_half = jnp.where(
        row < shifted, turned_rows, jnp.where(row > shifted, turned_mirrored, diagonal)
    )
    bottom = jnp.where(col < half, below, last_half)
    return jnp.concatenate([top, bottom], axis=0)


def partials_kernel(
    rows_hbm,
    grad_hbm,
    gain_hbm,
    sketch_hbm,
    copies_ref,
    out_ref,
    rows_ref,
    grad_ref,
    gain_ref,
    sketch_ref,
    sems,
):
    tokens, width = rows_ref.shape
    rank = sketch_ref.shape[0]
    chunk = width // CHUNKS
    small = [
        pltpu.make_async_copy(sketch_hbm, sketch_ref, sems.at[2 * CHUNKS]),
        pltpu.make_async_copy(gain_hbm, gain_ref, sems.at[2 * CHUNKS + 1]),
    ]
    large = []
    for turn, (source, target) in enumerate(((rows_hbm, rows_ref), (grad_hbm, grad_ref))):
        for i in range(CHUNKS):
            at = pl.ds(i * chunk, chunk)
            large.append(
                pltpu.make_async_copy(
                    source.at[:, at], target.at[:, at], sems.at[turn * CHUNKS + i]
                )
            )
    for copy in small + large:
        copy.start()
    for copy in small:
        copy.wait()
    totals = []
    for turn in range(2):
        total = None
        for i in range(CHUNKS):
            at = slice(i * chunk, (i + 1) * chunk)
            large[turn * CHUNKS + i].wait()
            if turn == 0:
                block = rows_ref[:, at]
            else:
                block = grad_ref[:, at].astype(F32) * gain_ref[:, at].astype(F32)
                block = block.astype(BF16)
            product = [
                lax.dot_general(left, block, CONTRACT_LAST, preferred_element_type=F32)
                for left in (block, sketch_ref[:, at])
            ]
            total = product if total is None else [a + b for a, b in zip(total, product)]
        totals.append(total)
    half = tokens // 2
    row, col = indices((tokens, tokens))
    diagonals = []
    for turn, (gram, first) in enumerate(totals):
        out_ref[turn * half : (turn + 1) * half] = packed(gram).astype(BF16)
        at = 2 * half + turn * rank
        out_ref[at : at + rank] = first.astype(BF16)
        diagonal = jnp.sum(jnp.where(row == col, gram, 0.0), axis=0, keepdims=True)
        high = diagonal.astype(BF16).astype(F32)
        diagonals += [high, diagonal - high]
    rest = jnp.zeros((out_ref.shape[0] - 2 * half - 2 * rank - 4, tokens), F32)
    tail = jnp.concatenate(diagonals + [rest], axis=0)
    out_ref[2 * half + 2 * rank :] = tail.astype(BF16)
    for copy in range(copies_ref.shape[0]):
        copies_ref[copy] = out_ref[...]


def orthonormal(gram, first):
    rank, _ = first.shape
    sketch = lax.dot_general(
        first, gram, (((1,), (0,)), ((), ())), precision=HIGHEST, preferred_element_type=F32
    )
    small = lax.dot_general(
        sketch, sketch, CONTRACT_LAST, precision=HIGHEST, preferred_element_type=F32
    )
    row, col = indices((rank, rank))
    trace = jnp.sum(jnp.where(row == col, small, 0.0), keepdims=True)
    small = small + jnp.where(row == col, trace * (RIDGE / rank), 0.0)
    return sketch, small


def eliminate(pairs):
    rank, tokens = pairs[0][0].shape
    states = [
        jnp.concatenate(
            [sketch, small, jnp.zeros((rank, tokens - rank), F32)], axis=1
        )
        for sketch, small in pairs
    ]
    done = [[] for _ in pairs]
    for start in range(0, rank, BLOCK):
        spread = [
            [
                jnp.broadcast_to(
                    state[:, tokens + k : tokens + k + 1], (rank, tokens)
                )
                for k in range(start, start + BLOCK)
            ]
            for state in states
        ]
        for j in range(BLOCK):
            k = start + j
            for n, columns in enumerate(spread):
                column = columns[j]
                pivot = column[k : k + 1]
                inverse = 1.0 / pivot
                inverse2 = jnp.concatenate([inverse, inverse], axis=1)
                row = states[n][k : k + 1]
                scale = lax.rsqrt(pivot)
                scale = scale * (1.5 - 0.5 * pivot * scale * scale)
                done[n].append(row[:, :tokens] * scale)
                column2 = jnp.concatenate([column, column], axis=1)
                states[n] = states[n] - column2 * (row * inverse2)
                for m in range(j + 1, BLOCK):
                    other = column[start + m : start + m + 1] * inverse
                    columns[m] = columns[m] - column * other
    return [jnp.concatenate(finished, axis=0) for finished in done]


def factor_kernel(
    gathered_ref, rows_hbm, next_hbm, spread_ref, backward_ref, local_ref, rows_ref, next_ref, sems
):
    copies = [
        pltpu.make_async_copy(rows_hbm, rows_ref, sems.at[0]),
        pltpu.make_async_copy(next_hbm, next_ref, sems.at[1]),
    ]
    for copy in copies:
        copy.start()
    tokens, width = rows_ref.shape
    rank = backward_ref.shape[0]
    half = tokens // 2
    total = gathered_ref[0].astype(F32)
    for member in range(1, gathered_ref.shape[0]):
        total = total + gathered_ref[member].astype(F32)
    pairs = []
    for turn in range(2):
        at = 2 * half + turn * rank
        mark = 2 * half + 2 * rank + 2 * turn
        diagonal = total[mark : mark + 1] + total[mark + 1 : mark + 2]
        gram = unpacked(total[turn * half : (turn + 1) * half], diagonal)
        pairs.append(orthonormal(gram, total[at : at + rank]))
    forward, backward = (basis.astype(BF16) for basis in eliminate(pairs))
    backward_ref[...] = backward
    for copy in copies:
        copy.wait()
    chunk = 1024
    for start in range(0, width, chunk):
        coeff = jnp.dot(
            forward, rows_ref[:, start : start + chunk], preferred_element_type=F32
        ).astype(BF16)
        other = jnp.dot(forward, next_ref[:, start : start + chunk], preferred_element_type=F32)
        summed = jnp.sum(coeff.astype(F32) * other, axis=0, keepdims=True)
        for lane in range(0, chunk, 128):
            at = (start + lane) // 128
            local_ref[at : at + 1] = summed[:, lane : lane + 128]
    local = local_ref[...].astype(BF16)
    for i in range(spread_ref.shape[0]):
        spread_ref[i] = local


def coeff_kernel(basis_ref, grad_ref, gain_ref, out_ref):
    width = grad_ref.shape[1]
    basis = basis_ref[...]
    gained = (grad_ref[...].astype(F32) * gain_ref[...].astype(F32)).astype(BF16)
    out_ref[:, :width] = jnp.dot(basis, gained, preferred_element_type=F32).astype(BF16)
    out_ref[:, width:] = basis


def rebuild_kernel(both_ref, out_hbm, out_ref, sems):
    _, width = out_ref.shape
    basis = both_ref[:, width:].T
    chunk = width // CHUNKS
    copies = []
    for i in range(CHUNKS):
        at = i * chunk
        out_ref[:, at : at + chunk] = jnp.dot(
            basis, both_ref[:, at : at + chunk], preferred_element_type=F32
        ).astype(BF16)
        window = pl.ds(at, chunk)
        copies.append(
            pltpu.make_async_copy(out_ref.at[:, window], out_hbm.at[:, window], sems.at[i])
        )
        copies[-1].start()
    for copy in copies:
        copy.wait()


def partials(rows, grad, gain, sketch_rows, copies):
    tokens, width = rows.shape
    rank = sketch_rows.shape[0]
    anywhere = pl.BlockSpec(memory_space=pl.ANY)
    return pl.pallas_call(
        partials_kernel,
        out_shape=jax.ShapeDtypeStruct((copies, tokens + 2 * rank + 8, tokens), BF16),
        in_specs=[anywhere] * 4,
        out_specs=pl.BlockSpec(memory_space=pltpu.VMEM),
        scratch_shapes=[
            pltpu.VMEM((tokens + 2 * rank + 8, tokens), BF16),
            pltpu.VMEM((tokens, width), BF16),
            pltpu.VMEM((tokens, width), BF16),
            pltpu.VMEM((1, width), BF16),
            pltpu.VMEM((rank, width), BF16),
            pltpu.SemaphoreType.DMA((2 * CHUNKS + 2,)),
        ],
        name="partials",
    )(rows, grad, gain, sketch_rows)


def factors(gathered, rows, next_grad, rank, copies):
    tokens, width = rows.shape
    vmem = pl.BlockSpec(memory_space=pltpu.VMEM)
    anywhere = pl.BlockSpec(memory_space=pl.ANY)
    basis = jax.ShapeDtypeStruct((rank, tokens), BF16)
    return pl.pallas_call(
        factor_kernel,
        out_shape=(jax.ShapeDtypeStruct((copies, width // 128, 128), BF16), basis),
        in_specs=[vmem, anywhere, anywhere],
        out_specs=(vmem, vmem),
        scratch_shapes=[
            pltpu.VMEM((width // 128, 128), F32),
            pltpu.VMEM((tokens, width), BF16),
            pltpu.VMEM((tokens, width), BF16),
            pltpu.SemaphoreType.DMA((2,)),
        ],
        compiler_params=SMALL,
        name="factors",
    )(gathered, rows, next_grad)


def coefficients(basis, grad, gain):
    rank, tokens = basis.shape
    width = grad.shape[1]
    vmem = pl.BlockSpec(memory_space=pltpu.VMEM)
    return pl.pallas_call(
        coeff_kernel,
        out_shape=jax.ShapeDtypeStruct((rank, width + tokens), BF16),
        in_specs=[vmem, vmem, vmem],
        out_specs=vmem,
        compiler_params=SMALL,
        name="coefficients",
    )(basis, grad, gain)


def rebuild(both, tokens):
    width = both.shape[1] - tokens
    return pl.pallas_call(
        rebuild_kernel,
        out_shape=jax.ShapeDtypeStruct((tokens, width), BF16),
        in_specs=[pl.BlockSpec(memory_space=pltpu.VMEM)],
        out_specs=pl.BlockSpec(memory_space=pl.ANY),
        scratch_shapes=[
            pltpu.VMEM((tokens, width), BF16),
            pltpu.SemaphoreType.DMA((CHUNKS,)),
        ],
        compiler_params=SMALL,
        name="rebuild",
    )(both)


def along_section(block, distance):
    devices = range(lax.axis_size("section"))
    route = [(i, i + distance) for i in devices if i + distance in devices]
    return lax.ppermute(block, "section", route)


def shards(section_output, sketch_matrix, boundary_gain, grad_gained):
    rows = section_output[0]
    sketch_rows = sketch_matrix[0].T
    grad = grad_gained[0]
    tokens = rows.shape[0]
    next_grad = along_section(grad, -1)
    members = lax.axis_size("tensor")
    mine = partials(rows, grad, boundary_gain, sketch_rows, members)
    gathered = lax.all_to_all(mine, "tensor", 0, 0)
    local, backward = factors(
        gathered, rows, next_grad, sketch_rows.shape[0], lax.axis_size("dp")
    )
    both = coefficients(backward, grad, boundary_gain)
    both = along_section(both, -1)
    locals_ = lax.all_to_all(local, "dp", 0, 0)
    summed = jnp.sum(locals_.astype(F32), axis=0)
    gain_grad = along_section(summed, 1)
    grad_output = rebuild(both, tokens)
    return grad_output[None], gain_grad.reshape(1, -1)


def solution(mesh):
    return jax.shard_map(
        shards,
        mesh=mesh,
        in_specs=(
            P("section", "dp", "tensor"),
            P("section", "tensor", None),
            P("section", "tensor"),
            P("section", "dp", "tensor"),
        ),
        out_specs=(P("section", "dp", "tensor"), P("section", "tensor")),
        check_vma=False,
    )
```

```python
import jax
import jax.numpy as jnp
from jax import lax
from jax.experimental import pallas as pl
from jax.experimental.pallas import tpu as pltpu
from jax.sharding import PartitionSpec as P


F32 = jnp.float32
BF16 = jnp.bfloat16
HIGHEST = lax.Precision.HIGHEST
RIDGE = 1e-06
CHUNKS = 4
BLOCK = 4
SMALL = pltpu.CompilerParams(vmem_limit_bytes=16 * 1024 * 1024)
CONTRACT_LAST = (((1,), (1,)), ((), ()))


def indices(shape):
    return (
        lax.broadcasted_iota(jnp.int32, shape, 0),
        lax.broadcasted_iota(jnp.int32, shape, 1),
    )


def packed(gram):
    half = gram.shape[0] // 2
    row, col = indices((half, 2 * half))
    turned = pltpu.roll(gram[half:], half, 1)
    return jnp.where((col < half) & (col >= row), turned, gram[:half])


def unpacked(rows, diagonal):
    half = rows.shape[0]
    row, col = indices((half, 2 * half))
    square = jnp.concatenate([rows, jnp.zeros_like(rows)], axis=0).T
    mirrored, below = square[:half], square[half:]
    first_half = jnp.where(row > col, rows, jnp.where(row < col, mirrored, diagonal))
    top = jnp.where(col < half, first_half, rows)
    shifted = col - half
    turned_rows = pltpu.roll(rows, half, 1)
    turned_mirrored = pltpu.roll(mirrored, half, 1)
    last_half = jnp.where(
        row < shifted, turned_rows, jnp.where(row > shifted, turned_mirrored, diagonal)
    )
    bottom = jnp.where(col < half, below, last_half)
    return jnp.concatenate([top, bottom], axis=0)


def partials_kernel(
    rows_hbm, grad_hbm, gain_hbm, sketch_hbm, out_ref, rows_ref, grad_ref, gain_ref, sketch_ref, sems
):
    tokens, width = rows_ref.shape
    rank = sketch_ref.shape[0]
    chunk = width // CHUNKS
    small = [
        pltpu.make_async_copy(sketch_hbm, sketch_ref, sems.at[2 * CHUNKS]),
        pltpu.make_async_copy(gain_hbm, gain_ref, sems.at[2 * CHUNKS + 1]),
    ]
    large = []
    for turn, (source, target) in enumerate(((rows_hbm, rows_ref), (grad_hbm, grad_ref))):
        for i in range(CHUNKS):
            at = pl.ds(i * chunk, chunk)
            large.append(
                pltpu.make_async_copy(
                    source.at[:, at], target.at[:, at], sems.at[turn * CHUNKS + i]
                )
            )
    for copy in small + large:
        copy.start()
    for copy in small:
        copy.wait()
    totals = []
    for turn in range(2):
        total = None
        for i in range(CHUNKS):
            at = slice(i * chunk, (i + 1) * chunk)
            large[turn * CHUNKS + i].wait()
            if turn == 0:
                block = rows_ref[:, at]
            else:
                block = grad_ref[:, at].astype(F32) * gain_ref[:, at].astype(F32)
                block = block.astype(BF16)
            product = [
                lax.dot_general(left, block, CONTRACT_LAST, preferred_element_type=F32)
                for left in (block, sketch_ref[:, at])
            ]
            total = product if total is None else [a + b for a, b in zip(total, product)]
        totals.append(total)
    half = tokens // 2
    row, col = indices((tokens, tokens))
    diagonals = []
    for turn, (gram, first) in enumerate(totals):
        out_ref[turn * half : (turn + 1) * half] = packed(gram).astype(BF16)
        at = 2 * half + turn * rank
        out_ref[at : at + rank] = first.astype(BF16)
        diagonal = jnp.sum(jnp.where(row == col, gram, 0.0), axis=0, keepdims=True)
        high = diagonal.astype(BF16).astype(F32)
        diagonals += [high, diagonal - high]
    rest = jnp.zeros((out_ref.shape[0] - 2 * half - 2 * rank - 4, tokens), F32)
    tail = jnp.concatenate(diagonals + [rest], axis=0)
    out_ref[2 * half + 2 * rank :] = tail.astype(BF16)


def orthonormal(gram, first):
    rank, _ = first.shape
    sketch = lax.dot_general(
        first, gram, (((1,), (0,)), ((), ())), precision=HIGHEST, preferred_element_type=F32
    )
    small = lax.dot_general(
        sketch, sketch, CONTRACT_LAST, precision=HIGHEST, preferred_element_type=F32
    )
    row, col = indices((rank, rank))
    trace = jnp.sum(jnp.where(row == col, small, 0.0), keepdims=True)
    small = small + jnp.where(row == col, trace * (RIDGE / rank), 0.0)
    return sketch, small


def eliminate(pairs):
    rank, tokens = pairs[0][0].shape
    states = [
        jnp.concatenate(
            [sketch, small, jnp.zeros((rank, tokens - rank), F32)], axis=1
        )
        for sketch, small in pairs
    ]
    done = [[] for _ in pairs]
    for start in range(0, rank, BLOCK):
        spread = [
            [
                jnp.broadcast_to(
                    state[:, tokens + k : tokens + k + 1], (rank, tokens)
                )
                for k in range(start, start + BLOCK)
            ]
            for state in states
        ]
        for j in range(BLOCK):
            k = start + j
            for n, columns in enumerate(spread):
                column = columns[j]
                pivot = column[k : k + 1]
                inverse = 1.0 / pivot
                inverse2 = jnp.concatenate([inverse, inverse], axis=1)
                row = states[n][k : k + 1]
                scale = lax.rsqrt(pivot)
                scale = scale * (1.5 - 0.5 * pivot * scale * scale)
                done[n].append(row[:, :tokens] * scale)
                column2 = jnp.concatenate([column, column], axis=1)
                states[n] = states[n] - column2 * (row * inverse2)
                for m in range(j + 1, BLOCK):
                    other = column[start + m : start + m + 1] * inverse
                    columns[m] = columns[m] - column * other
    return [jnp.concatenate(finished, axis=0) for finished in done]


def factor_kernel(gathered_ref, forward_ref, backward_ref):
    rank, tokens = forward_ref.shape
    half = tokens // 2
    total = gathered_ref[0].astype(F32)
    for member in range(1, gathered_ref.shape[0]):
        total = total + gathered_ref[member].astype(F32)
    pairs = []
    for turn in range(2):
        at = 2 * half + turn * rank
        mark = 2 * half + 2 * rank + 2 * turn
        diagonal = total[mark : mark + 1] + total[mark + 1 : mark + 2]
        gram = unpacked(total[turn * half : (turn + 1) * half], diagonal)
        pairs.append(orthonormal(gram, total[at : at + rank]))
    forward, backward = eliminate(pairs)
    forward_ref[...] = forward.astype(BF16)
    backward_ref[...] = backward.astype(BF16)


def local_kernel(basis_ref, rows_ref, grad_ref, spread_ref, local_ref):
    width = rows_ref.shape[1]
    basis = basis_ref[...]
    chunk = 1024
    for start in range(0, width, chunk):
        at = slice(start, start + chunk)
        coeff = jnp.dot(basis, rows_ref[:, at], preferred_element_type=F32).astype(BF16)
        other = jnp.dot(basis, grad_ref[:, at], preferred_element_type=F32)
        summed = jnp.sum(coeff.astype(F32) * other, axis=0, keepdims=True)
        for lane in range(0, chunk, 128):
            line = (start + lane) // 128
            local_ref[line : line + 1] = summed[:, lane : lane + 128]
    local = local_ref[...].astype(BF16)
    for i in range(spread_ref.shape[0]):
        spread_ref[i] = local


def coeff_kernel(basis_ref, grad_ref, gain_ref, out_ref):
    width = grad_ref.shape[1]
    basis = basis_ref[...]
    gained = (grad_ref[...].astype(F32) * gain_ref[...].astype(F32)).astype(BF16)
    out_ref[:, :width] = jnp.dot(basis, gained, preferred_element_type=F32).astype(BF16)
    out_ref[:, width:] = basis


def rebuild_kernel(both_ref, out_hbm, out_ref, sems):
    _, width = out_ref.shape
    basis = both_ref[:, width:].T
    chunk = width // CHUNKS
    copies = []
    for i in range(CHUNKS):
        at = i * chunk
        out_ref[:, at : at + chunk] = jnp.dot(
            basis, both_ref[:, at : at + chunk], preferred_element_type=F32
        ).astype(BF16)
        window = pl.ds(at, chunk)
        copies.append(
            pltpu.make_async_copy(out_ref.at[:, window], out_hbm.at[:, window], sems.at[i])
        )
        copies[-1].start()
    for copy in copies:
        copy.wait()


def partials(rows, grad, gain, sketch_rows):
    tokens, width = rows.shape
    rank = sketch_rows.shape[0]
    anywhere = pl.BlockSpec(memory_space=pl.ANY)
    return pl.pallas_call(
        partials_kernel,
        out_shape=jax.ShapeDtypeStruct((tokens + 2 * rank + 8, tokens), BF16),
        in_specs=[anywhere] * 4,
        out_specs=pl.BlockSpec(memory_space=pltpu.VMEM),
        scratch_shapes=[
            pltpu.VMEM((tokens, width), BF16),
            pltpu.VMEM((tokens, width), BF16),
            pltpu.VMEM((1, width), BF16),
            pltpu.VMEM((rank, width), BF16),
            pltpu.SemaphoreType.DMA((2 * CHUNKS + 2,)),
        ],
        name="partials",
    )(rows, grad, gain, sketch_rows)


def factors(gathered, rank):
    tokens = gathered.shape[2]
    vmem = pl.BlockSpec(memory_space=pltpu.VMEM)
    basis = jax.ShapeDtypeStruct((rank, tokens), BF16)
    return pl.pallas_call(
        factor_kernel,
        out_shape=(basis, basis),
        in_specs=[vmem],
        out_specs=(vmem, vmem),
        compiler_params=SMALL,
        name="factors",
    )(gathered)


def local_sums(basis, rows, grad, copies):
    width = rows.shape[1]
    vmem = pl.BlockSpec(memory_space=pltpu.VMEM)
    return pl.pallas_call(
        local_kernel,
        out_shape=jax.ShapeDtypeStruct((copies, width // 128, 128), BF16),
        in_specs=[vmem, vmem, vmem],
        out_specs=vmem,
        scratch_shapes=[pltpu.VMEM((width // 128, 128), F32)],
        compiler_params=SMALL,
        name="local_sums",
    )(basis, rows, grad)


def coefficients(basis, grad, gain):
    rank, tokens = basis.shape
    width = grad.shape[1]
    vmem = pl.BlockSpec(memory_space=pltpu.VMEM)
    return pl.pallas_call(
        coeff_kernel,
        out_shape=jax.ShapeDtypeStruct((rank, width + tokens), BF16),
        in_specs=[vmem, vmem, vmem],
        out_specs=vmem,
        compiler_params=SMALL,
        name="coefficients",
    )(basis, grad, gain)


def rebuild(both, tokens):
    width = both.shape[1] - tokens
    return pl.pallas_call(
        rebuild_kernel,
        out_shape=jax.ShapeDtypeStruct((tokens, width), BF16),
        in_specs=[pl.BlockSpec(memory_space=pltpu.VMEM)],
        out_specs=pl.BlockSpec(memory_space=pl.ANY),
        scratch_shapes=[
            pltpu.VMEM((tokens, width), BF16),
            pltpu.SemaphoreType.DMA((CHUNKS,)),
        ],
        compiler_params=SMALL,
        name="rebuild",
    )(both)


def along_section(block, distance):
    devices = range(lax.axis_size("section"))
    route = [(i, i + distance) for i in devices if i + distance in devices]
    return lax.ppermute(block, "section", route)


def shards(section_output, sketch_matrix, boundary_gain, grad_gained):
    rows = section_output[0]
    sketch_rows = sketch_matrix[0].T
    grad = grad_gained[0]
    tokens = rows.shape[0]
    earlier_rows = along_section(rows, 1)
    mine = partials(rows, grad, boundary_gain, sketch_rows)
    gathered = lax.all_gather(mine, "tensor")
    forward, backward = factors(gathered, sketch_rows.shape[0])
    forward = along_section(forward, 1)
    both = coefficients(backward, grad, boundary_gain)
    both = along_section(both, -1)
    local = local_sums(forward, earlier_rows, grad, lax.axis_size("dp"))
    parts = lax.all_to_all(local, "dp", 0, 0)
    gain_grad = jnp.sum(parts.astype(F32), axis=0)
    grad_output = rebuild(both, tokens)
    return grad_output[None], gain_grad.reshape(1, -1)


def solution(mesh):
    return jax.shard_map(
        shards,
        mesh=mesh,
        in_specs=(
            P("section", "dp", "tensor"),
            P("section", "tensor", None),
            P("section", "tensor"),
            P("section", "dp", "tensor"),
        ),
        out_specs=(P("section", "dp", "tensor"), P("section", "tensor")),
        check_vma=False,
    )
```

```python
import jax
import jax.numpy as jnp
from jax import lax
from jax.experimental import pallas as pl
from jax.experimental.pallas import tpu as pltpu
from jax.sharding import PartitionSpec as P


F32 = jnp.float32
BF16 = jnp.bfloat16
HIGHEST = lax.Precision.HIGHEST
RIDGE = 1e-06
CHUNKS = 4
BLOCK = 4
SMALL = pltpu.CompilerParams(vmem_limit_bytes=16 * 1024 * 1024)
CONTRACT_LAST = (((1,), (1,)), ((), ()))


def indices(shape):
    return (
        lax.broadcasted_iota(jnp.int32, shape, 0),
        lax.broadcasted_iota(jnp.int32, shape, 1),
    )


def packed(gram):
    half = gram.shape[0] // 2
    row, col = indices((half, 2 * half))
    turned = pltpu.roll(gram[half:], half, 1)
    return jnp.where((col < half) & (col >= row), turned, gram[:half])


def unpacked(rows, diagonal):
    half = rows.shape[0]
    row, col = indices((half, 2 * half))
    square = jnp.concatenate([rows, jnp.zeros_like(rows)], axis=0).T
    mirrored, below = square[:half], square[half:]
    first_half = jnp.where(row > col, rows, jnp.where(row < col, mirrored, diagonal))
    top = jnp.where(col < half, first_half, rows)
    shifted = col - half
    turned_rows = pltpu.roll(rows, half, 1)
    turned_mirrored = pltpu.roll(mirrored, half, 1)
    last_half = jnp.where(
        row < shifted, turned_rows, jnp.where(row > shifted, turned_mirrored, diagonal)
    )
    bottom = jnp.where(col < half, below, last_half)
    return jnp.concatenate([top, bottom], axis=0)


def partials_kernel(
    rows_hbm,
    grad_hbm,
    gain_hbm,
    sketch_hbm,
    forward_ref,
    backward_ref,
    rows_ref,
    grad_ref,
    gain_ref,
    sketch_ref,
    sems,
):
    tokens, width = rows_ref.shape
    rank = sketch_ref.shape[0]
    chunk = width // CHUNKS
    small = [
        pltpu.make_async_copy(sketch_hbm, sketch_ref, sems.at[2 * CHUNKS]),
        pltpu.make_async_copy(gain_hbm, gain_ref, sems.at[2 * CHUNKS + 1]),
    ]
    large = []
    for turn, (source, target) in enumerate(((rows_hbm, rows_ref), (grad_hbm, grad_ref))):
        for i in range(CHUNKS):
            at = pl.ds(i * chunk, chunk)
            large.append(
                pltpu.make_async_copy(
                    source.at[:, at], target.at[:, at], sems.at[turn * CHUNKS + i]
                )
            )
    for copy in small + large:
        copy.start()
    for copy in small:
        copy.wait()
    totals = []
    for turn in range(2):
        total = None
        for i in range(CHUNKS):
            at = slice(i * chunk, (i + 1) * chunk)
            large[turn * CHUNKS + i].wait()
            if turn == 0:
                block = rows_ref[:, at]
            else:
                block = grad_ref[:, at].astype(F32) * gain_ref[:, at].astype(F32)
                block = block.astype(BF16)
            product = [
                lax.dot_general(left, block, CONTRACT_LAST, preferred_element_type=F32)
                for left in (block, sketch_ref[:, at])
            ]
            total = product if total is None else [a + b for a, b in zip(total, product)]
        totals.append(total)
    half = tokens // 2
    row, col = indices((tokens, tokens))
    for out_ref, (gram, first) in zip((forward_ref, backward_ref), totals):
        diagonal = jnp.sum(jnp.where(row == col, gram, 0.0), axis=0, keepdims=True)
        high = diagonal.astype(BF16).astype(F32)
        rest = jnp.zeros((out_ref.shape[0] - half - rank - 2, tokens), F32)
        tail = jnp.concatenate([high, diagonal - high, rest], axis=0)
        out_ref[:half] = packed(gram).astype(BF16)
        out_ref[half : half + rank] = first.astype(BF16)
        out_ref[half + rank :] = tail.astype(BF16)


def orthonormal(gram, first):
    rank, _ = first.shape
    sketch = lax.dot_general(
        first, gram, (((1,), (0,)), ((), ())), precision=HIGHEST, preferred_element_type=F32
    )
    small = lax.dot_general(
        sketch, sketch, CONTRACT_LAST, precision=HIGHEST, preferred_element_type=F32
    )
    row, col = indices((rank, rank))
    trace = jnp.sum(jnp.where(row == col, small, 0.0), keepdims=True)
    small = small + jnp.where(row == col, trace * (RIDGE / rank), 0.0)
    return sketch, small


def eliminate(pairs):
    rank, tokens = pairs[0][0].shape
    states = [
        jnp.concatenate(
            [sketch, small, jnp.zeros((rank, tokens - rank), F32)], axis=1
        )
        for sketch, small in pairs
    ]
    done = [[] for _ in pairs]
    for start in range(0, rank, BLOCK):
        spread = [
            [
                jnp.broadcast_to(
                    state[:, tokens + k : tokens + k + 1], (rank, tokens)
                )
                for k in range(start, start + BLOCK)
            ]
            for state in states
        ]
        for j in range(BLOCK):
            k = start + j
            for n, columns in enumerate(spread):
                column = columns[j]
                pivot = column[k : k + 1]
                inverse = 1.0 / pivot
                inverse2 = jnp.concatenate([inverse, inverse], axis=1)
                row = states[n][k : k + 1]
                scale = lax.rsqrt(pivot)
                scale = scale * (1.5 - 0.5 * pivot * scale * scale)
                done[n].append(row[:, :tokens] * scale)
                column2 = jnp.concatenate([column, column], axis=1)
                states[n] = states[n] - column2 * (row * inverse2)
                for m in range(j + 1, BLOCK):
                    other = column[start + m : start + m + 1] * inverse
                    columns[m] = columns[m] - column * other
    return [jnp.concatenate(finished, axis=0) for finished in done]


def factor_kernel(gathered_ref, forward_ref, backward_ref):
    rank, tokens = forward_ref.shape
    half = tokens // 2
    total = gathered_ref[0].astype(F32)
    for member in range(1, gathered_ref.shape[0]):
        total = total + gathered_ref[member].astype(F32)
    pairs = []
    for turn in range(2):
        at = turn * (total.shape[0] // 2)
        mark = at + half + rank
        diagonal = total[mark : mark + 1] + total[mark + 1 : mark + 2]
        gram = unpacked(total[at : at + half], diagonal)
        pairs.append(orthonormal(gram, total[at + half : mark]))
    forward, backward = eliminate(pairs)
    forward_ref[...] = forward.astype(BF16)
    backward_ref[...] = backward.astype(BF16)


def local_kernel(basis_ref, rows_ref, grad_ref, spread_ref, local_ref):
    width = rows_ref.shape[1]
    basis = basis_ref[...]
    chunk = 1024
    for start in range(0, width, chunk):
        at = slice(start, start + chunk)
        coeff = jnp.dot(basis, rows_ref[:, at], preferred_element_type=F32).astype(BF16)
        other = jnp.dot(basis, grad_ref[:, at], preferred_element_type=F32)
        summed = jnp.sum(coeff.astype(F32) * other, axis=0, keepdims=True)
        for lane in range(0, chunk, 128):
            line = (start + lane) // 128
            local_ref[line : line + 1] = summed[:, lane : lane + 128]
    local = local_ref[...].astype(BF16)
    for i in range(spread_ref.shape[0]):
        spread_ref[i] = local


def coeff_kernel(basis_ref, grad_ref, gain_ref, out_ref):
    width = grad_ref.shape[1]
    basis = basis_ref[...]
    gained = (grad_ref[...].astype(F32) * gain_ref[...].astype(F32)).astype(BF16)
    out_ref[:, :width] = jnp.dot(basis, gained, preferred_element_type=F32).astype(BF16)
    out_ref[:, width:] = basis


def rebuild_kernel(both_ref, out_hbm, out_ref, sems):
    _, width = out_ref.shape
    basis = both_ref[:, width:].T
    chunk = width // CHUNKS
    copies = []
    for i in range(CHUNKS):
        at = i * chunk
        out_ref[:, at : at + chunk] = jnp.dot(
            basis, both_ref[:, at : at + chunk], preferred_element_type=F32
        ).astype(BF16)
        window = pl.ds(at, chunk)
        copies.append(
            pltpu.make_async_copy(out_ref.at[:, window], out_hbm.at[:, window], sems.at[i])
        )
        copies[-1].start()
    for copy in copies:
        copy.wait()


def partials(rows, grad, gain, sketch_rows):
    tokens, width = rows.shape
    rank = sketch_rows.shape[0]
    anywhere = pl.BlockSpec(memory_space=pl.ANY)
    vmem = pl.BlockSpec(memory_space=pltpu.VMEM)
    out = jax.ShapeDtypeStruct((tokens // 2 + rank + 8, tokens), BF16)
    return pl.pallas_call(
        partials_kernel,
        out_shape=(out, out),
        in_specs=[anywhere] * 4,
        out_specs=(vmem, vmem),
        scratch_shapes=[
            pltpu.VMEM((tokens, width), BF16),
            pltpu.VMEM((tokens, width), BF16),
            pltpu.VMEM((1, width), BF16),
            pltpu.VMEM((rank, width), BF16),
            pltpu.SemaphoreType.DMA((2 * CHUNKS + 2,)),
        ],
        compiler_params=pltpu.CompilerParams(vmem_limit_bytes=55000 * 1024),
        name="partials",
    )(rows, grad, gain, sketch_rows)


def factors(gathered, rank):
    tokens = gathered.shape[2]
    vmem = pl.BlockSpec(memory_space=pltpu.VMEM)
    basis = jax.ShapeDtypeStruct((rank, tokens), BF16)
    return pl.pallas_call(
        factor_kernel,
        out_shape=(basis, basis),
        in_specs=[vmem],
        out_specs=(vmem, vmem),
        compiler_params=SMALL,
        name="factors",
    )(gathered)


def local_sums(basis, rows, grad, copies):
    width = rows.shape[1]
    vmem = pl.BlockSpec(memory_space=pltpu.VMEM)
    return pl.pallas_call(
        local_kernel,
        out_shape=jax.ShapeDtypeStruct((copies, width // 128, 128), BF16),
        in_specs=[vmem, vmem, vmem],
        out_specs=vmem,
        scratch_shapes=[pltpu.VMEM((width // 128, 128), F32)],
        compiler_params=SMALL,
        name="local_sums",
    )(basis, rows, grad)


def coefficients(basis, grad, gain):
    rank, tokens = basis.shape
    width = grad.shape[1]
    vmem = pl.BlockSpec(memory_space=pltpu.VMEM)
    return pl.pallas_call(
        coeff_kernel,
        out_shape=jax.ShapeDtypeStruct((rank, width + tokens), BF16),
        in_specs=[vmem, vmem, vmem],
        out_specs=vmem,
        compiler_params=SMALL,
        name="coefficients",
    )(basis, grad, gain)


def rebuild(both, tokens):
    width = both.shape[1] - tokens
    return pl.pallas_call(
        rebuild_kernel,
        out_shape=jax.ShapeDtypeStruct((tokens, width), BF16),
        in_specs=[pl.BlockSpec(memory_space=pltpu.VMEM)],
        out_specs=pl.BlockSpec(memory_space=pl.ANY),
        scratch_shapes=[
            pltpu.VMEM((tokens, width), BF16),
            pltpu.SemaphoreType.DMA((CHUNKS,)),
        ],
        compiler_params=SMALL,
        name="rebuild",
    )(both)


def along_section(block, distance):
    devices = range(lax.axis_size("section"))
    route = [(i, i + distance) for i in devices if i + distance in devices]
    return lax.ppermute(block, "section", route)


def shards(section_output, sketch_matrix, boundary_gain, grad_gained):
    rows = section_output[0]
    sketch_rows = sketch_matrix[0].T
    grad = grad_gained[0]
    tokens = rows.shape[0]
    earlier_rows = along_section(rows, 1)
    forward_part, backward_part = partials(rows, grad, boundary_gain, sketch_rows)
    forward_part = along_section(forward_part, 1)
    mine = jnp.concatenate([forward_part, backward_part], axis=0)
    gathered = lax.all_gather(mine, "tensor")
    forward, backward = factors(gathered, sketch_rows.shape[0])
    local = local_sums(forward, earlier_rows, grad, lax.axis_size("dp"))
    parts = lax.all_to_all(local, "dp", 0, 0)
    both = coefficients(backward, grad, boundary_gain)
    both = along_section(both, -1)
    gain_grad = jnp.sum(parts.astype(F32), axis=0)
    gain_grad = jnp.where(lax.axis_index("section") == 0, 0.0, gain_grad)
    grad_output = rebuild(both, tokens)
    return grad_output[None], gain_grad.reshape(1, -1)


def solution(mesh):
    return jax.shard_map(
        shards,
        mesh=mesh,
        in_specs=(
            P("section", "dp", "tensor"),
            P("section", "tensor", None),
            P("section", "tensor"),
            P("section", "dp", "tensor"),
        ),
        out_specs=(P("section", "dp", "tensor"), P("section", "tensor")),
        check_vma=False,
    )
```
